32 devices in a mesh: pipe: 2 (over core), ctx: 8 (over z, x), tp: 2 (over y).
Axes of the slice: x: 2, y: 2, z: 4, core: 2. Of those that a mesh axis runs over, the one named last changes fastest.
Arguments:
- tokens: bfloat16 [1, 1024, 4096], P(None, ('ctx', 'tp')), may hold values from -6 to 6
- norm_gain: bfloat16 [2, 4096], P('pipe'), may hold values from 0.099609375 to 1.8984375
- query_weight: bfloat16 [2, 4096, 4096], P('pipe', 'ctx', 'tp'), may hold values from -0.1875 to 0.1875
- keyval_weight: bfloat16 [2, 4096, 2048], P('pipe', None, 'tp'), may hold values from -0.1875 to 0.1875
- output_weight: bfloat16 [2, 4096, 4096], P('pipe', 'tp', 'ctx'), may hold values from -0.09375 to 0.09375
Outputs:
- states: bfloat16 [2, 1, 1024, 4096], P('pipe', None, ('ctx', 'tp'))
The draws below stay inside these ranges and needn't reach their ends.
All inputs are finite; a program needn't handle non-finite values.
Results may differ from the reference program's by a relative error of at most 0.033.
Values may be sent and summed in bfloat16 or wider, within the bound.
A program may use at most 192 MiB of HBM per device.

```python
import math
import jax
import jax.numpy as jnp
from jax import lax

D = 4096
HEADS = 32
KV_HEADS = 8
HEAD_DIM = 128
MICRO = 1
SEQ = 1024
LAYERS = 2
N_TP = 2


def levels(rng, shape, cuts, low, high):
    def one(axis_at, blocks):
        draws = jax.random.uniform(jax.random.fold_in(jax.random.fold_in(rng, 6), axis_at), (blocks,), jnp.float32, low / len(cuts), high / len(cuts))
        return jnp.repeat(jnp.exp(draws), shape[axis_at] // blocks).reshape((-1,) + (1,) * (len(shape) - axis_at - 1))

    level = one(*cuts[0])
    for cut in cuts[1:]:
        level = level * one(*cut)
    return level


def centred(stream_key, dims, spread, reach, cuts=(), kind=jnp.bfloat16):
    entries = jax.random.normal(stream_key, dims, jnp.float32) * spread
    if len(cuts) > 0:
        entries = levels(stream_key, dims, cuts, -0.22, 0.18) * entries
    return jnp.clip(entries, min=-reach, max=reach).astype(kind)


def setup_inputs(seed: int = 0) -> dict:
    seeds = jax.random.split(jax.random.key(seed), 6)
    return {
        "tokens": centred(seeds[0], (MICRO, SEQ, D), 1.0, 6.0, ((1, 16),)),
        "norm_gain": jnp.clip(1.0 + 0.18 * jax.random.normal(seeds[1], (LAYERS, D), jnp.float32), 0.099609375, 1.8984375).astype(jnp.bfloat16),
        "query_weight": centred(seeds[2], (LAYERS, D, HEADS * HEAD_DIM), (D // 4) ** -0.5, 0.1875, ((0, 2), (1, 8), (2, 2))),
        "keyval_weight": centred(seeds[3], (LAYERS, D, KV_HEADS * 2 * HEAD_DIM), (D // 4) ** -0.5, 0.1875, ((0, 2), (2, 2))),
        "output_weight": centred(seeds[4], (LAYERS, HEADS * HEAD_DIM, D), (HEADS * HEAD_DIM) ** -0.5, 0.09375, ((0, 2), (1, 2), (2, 8))),
    }


def rotate(field, positions):
    half = field.shape[-1] // 2
    freqs = 500000.0 ** (-jnp.arange(half, dtype=jnp.float32) * 2.0 / field.shape[-1])
    angles = positions.astype(jnp.float32)[:, None] * freqs[None, :]
    cosine = jnp.cos(angles)[:, None, :]
    sine = jnp.sin(angles)[:, None, :]
    first = field[..., :half]
    second = field[..., half:]
    return jnp.concatenate([first * cosine - second * sine, second * cosine + first * sine], axis=-1)

def normalize(block, scale_row):
    return (block * lax.rsqrt(lax.optimization_barrier(jnp.mean(block * block, axis=-1, keepdims=True)) + 1e-05) * scale_row).astype(jnp.bfloat16)

def attention(query, keys, values, positions):
    group = HEADS // KV_HEADS
    length = query.shape[0]
    grouped = query.reshape(length, KV_HEADS, group, HEAD_DIM).transpose(1, 2, 0, 3)
    key_major = keys.transpose(1, 0, 2)
    value_major = values.transpose(1, 0, 2)
    allowed = positions[None, :] <= positions[:, None]
    factor = 1.0 / math.sqrt(HEAD_DIM)

    def one_head(operands):
        head_query, head_keys, head_values = operands
        scores = jnp.einsum('gqd,kd->gqk', head_query.astype(jnp.float32), head_keys.astype(jnp.float32)) * factor
        scores = jnp.where(allowed[None], scores, -jnp.inf)
        peak = lax.optimization_barrier(jnp.max(scores, axis=-1, keepdims=True))
        weights = jnp.exp(scores - peak)
        total = lax.optimization_barrier(jnp.sum(weights, axis=-1, keepdims=True))
        rounded = lax.optimization_barrier(weights.astype(jnp.bfloat16)).astype(jnp.float32)
        mixed = jnp.einsum('gqk,kd->gqd', rounded, head_values.astype(jnp.float32))
        return mixed / total
    heads = lax.map(one_head, (grouped, key_major, value_major))
    return heads.transpose(2, 0, 1, 3).reshape(length, HEADS * HEAD_DIM).astype(jnp.bfloat16)

def layer(state, scale_row, query_weight, keyval_weight, output_weight, positions):
    length = state.shape[0]
    wide = state.astype(jnp.float32)
    normed = normalize(wide, scale_row.astype(jnp.float32))
    query = jnp.dot(normed, query_weight, preferred_element_type=jnp.float32).reshape(length, HEADS, HEAD_DIM)
    query = rotate(query, positions).astype(jnp.bfloat16)
    projected = jnp.dot(normed, keyval_weight, preferred_element_type=jnp.float32).reshape(length, KV_HEADS, 2, HEAD_DIM)
    keys = rotate(projected[:, :, 0], positions).astype(jnp.bfloat16)
    values = projected[:, :, 1].astype(jnp.bfloat16)
    attended = attention(query, keys, values, positions)
    per_group = HEADS * HEAD_DIM // N_TP

    def add_group(index, total):
        offset = (index * per_group).astype(jnp.int32)
        block = lax.dynamic_slice_in_dim(attended, offset, per_group, 1)
        weight_rows = lax.dynamic_slice_in_dim(output_weight, offset, per_group, 0)
        term = jnp.dot(block, weight_rows, preferred_element_type=jnp.float32).astype(jnp.bfloat16)
        return total + lax.optimization_barrier(term).astype(jnp.float32)
    summed = lax.fori_loop(0, N_TP, add_group, jnp.zeros((length, D), jnp.float32))
    return (wide + summed).astype(jnp.bfloat16)

def reference(tokens, norm_gain, query_weight, keyval_weight, output_weight):
    positions = jnp.arange(SEQ, dtype=jnp.int32)
    current = [tokens[index] for index in range(MICRO)]
    layered = []
    for depth in range(LAYERS):
        current = [layer(hidden, norm_gain[depth], query_weight[depth], keyval_weight[depth], output_weight[depth], positions) for hidden in current]
        layered.append(jnp.stack(current))
    return jnp.stack(layered)
```

```python
import math

import jax
import jax.numpy as jnp
from jax import lax
from jax.sharding import PartitionSpec as P

HEAD_DIM = 128


def shifted(value, axis, by):
    count = lax.axis_size(axis)
    pairs = [(i, i + by) for i in range(count) if 0 <= i + by < count]
    return lax.ppermute(value, axis, pairs)


def rotate(field, positions):
    half = field.shape[-1] // 2
    freqs = 500000.0 ** (-jnp.arange(half, dtype=jnp.float32) * 2.0 / field.shape[-1])
    angles = positions.astype(jnp.float32)[:, None] * freqs[None, :]
    cosine = jnp.cos(angles)[:, None, :]
    sine = jnp.sin(angles)[:, None, :]
    first = field[..., :half]
    second = field[..., half:]
    return jnp.concatenate(
        [first * cosine - second * sine, second * cosine + first * sine], axis=-1
    )


def normalize(block, scale_row):
    return (
        block * lax.rsqrt(jnp.mean(block * block, axis=-1, keepdims=True) + 1e-05) * scale_row
    ).astype(jnp.bfloat16)


def gathered(tokens, norm_gain, query_weight, keyval_weight, output_weight):
    segments = lax.axis_size("pipe")
    segment = lax.axis_index("pipe")
    tp_size = lax.axis_size("tp")
    ctx_pos = lax.axis_index("ctx")
    micro, rows, width = tokens.shape
    span = rows * tp_size
    scale_row = norm_gain[0].astype(jnp.float32)
    full_query, full_output = (
        lax.all_gather(query_weight[0], "ctx", axis=0, tiled=True),
        lax.all_gather(output_weight[0], "ctx", axis=1, tiled=True),
    )
    keyval = keyval_weight[0]
    q_count = full_query.shape[1] // HEAD_DIM
    kv_count = keyval.shape[1] // (2 * HEAD_DIM)
    group = q_count // kv_count
    positions = ctx_pos * span + jnp.arange(span, dtype=jnp.int32)
    factor = 1.0 / math.sqrt(HEAD_DIM)
    steps = micro + segments - 1
    received = jnp.zeros_like(tokens[0])
    results = []
    for step in range(steps):
        fresh = tokens[min(step, micro - 1)]
        state = jnp.where(segment == 0, fresh, received)
        wide = state.astype(jnp.float32)
        layer_normed = lax.all_gather(normalize(wide, scale_row), "tp", axis=0, tiled=True)
        query = jnp.dot(layer_normed, full_query, preferred_element_type=jnp.float32).reshape(
            span, q_count, HEAD_DIM
        )
        query = rotate(query, positions).astype(jnp.bfloat16)
        query = query.reshape(span, kv_count, group, HEAD_DIM).transpose(1, 2, 0, 3)
        projected = jnp.dot(layer_normed, keyval, preferred_element_type=jnp.float32).reshape(
            span, kv_count, 2, HEAD_DIM
        )
        keys = (
            rotate(projected[:, :, 0], positions)
            .astype(jnp.bfloat16)
            .reshape(span, kv_count * HEAD_DIM)
        )
        values = projected[:, :, 1].astype(jnp.bfloat16).reshape(span, kv_count * HEAD_DIM)
        piece = (
            lax.all_gather(keys, "ctx", axis=0, tiled=True),
            lax.all_gather(values, "ctx", axis=0, tiled=True),
        )
        run_max = jnp.full((kv_count, group, span), -1e30, jnp.float32)
        count = piece[0].shape[0]
        key_block = piece[0].reshape(count, kv_count, HEAD_DIM)
        value_block = piece[1].reshape(count, kv_count, HEAD_DIM)
        scores = (
            jnp.einsum("hgqd,khd->hgqk", query, key_block, preferred_element_type=jnp.float32)
            * factor
        )
        key_pos = jnp.arange(count, dtype=jnp.int32)
        allowed = key_pos[None, :] <= positions[:, None]
        scores = jnp.where(allowed, scores, -jnp.inf)
        new_max = jnp.maximum(run_max, jnp.max(scores, axis=-1))
        weights = jnp.exp(scores - new_max[..., None])
        total = jnp.sum(weights, axis=-1)
        mixed = jnp.einsum(
            "hgqk,khd->hgqd",
            weights.astype(jnp.bfloat16),
            value_block,
            preferred_element_type=jnp.float32,
        )
        run_max = new_max
        run_acc = mixed
        mixed = run_acc / total[..., None]
        attended = (
            mixed.transpose(2, 0, 1, 3).reshape(span, q_count * HEAD_DIM).astype(jnp.bfloat16)
        )
        summed = lax.psum_scatter(
            jnp.dot(attended, full_output, preferred_element_type=jnp.float32).astype(jnp.bfloat16),
            "tp",
            scatter_dimension=0,
            tiled=True,
        ).astype(jnp.float32)
        produced = (wide + summed).astype(jnp.bfloat16)
        results.append(produced)
        if step + 1 < steps:
            received = shifted(produced, "pipe", 1)
    stacked = jnp.stack(results)
    mine = lax.dynamic_slice_in_dim(stacked, segment, micro, 0)
    return mine[None]


def swap_halves(weight, axis):
    segments = lax.axis_size("pipe")
    shape = weight.shape
    split = shape[:axis] + (segments, shape[axis] // segments) + shape[axis + 1 :]
    blocks = jnp.moveaxis(weight.reshape(split), axis, 0)
    return lax.all_to_all(blocks, "pipe", 0, 0)


def attend(query, keys, values, positions):
    span, q_count, _ = query.shape
    kv_count = keys.shape[1]
    group = q_count // kv_count
    query = query.reshape(span, kv_count, group, HEAD_DIM).transpose(1, 2, 0, 3)
    scores = jnp.einsum("hgqd,khd->hgqk", query, keys, preferred_element_type=jnp.float32)
    scores = scores * (1.0 / math.sqrt(HEAD_DIM))
    allowed = jnp.arange(keys.shape[0], dtype=jnp.int32)[None, :] <= positions[:, None]
    scores = jnp.where(allowed, scores, -jnp.inf)
    weights = jnp.exp(scores - jnp.max(scores, axis=-1, keepdims=True))
    total = jnp.sum(weights, axis=-1, keepdims=True)
    mixed = jnp.einsum(
        "hgqk,khd->hgqd",
        weights.astype(jnp.bfloat16),
        values,
        preferred_element_type=jnp.float32,
    )
    mixed = (mixed / total).astype(jnp.bfloat16)
    return mixed.transpose(2, 0, 1, 3).reshape(span, q_count * HEAD_DIM)


def spread(tokens, norm_gain, query_weight, keyval_weight, output_weight):
    layers = lax.axis_size("pipe")
    tp_size = lax.axis_size("tp")
    ctx_size = lax.axis_size("ctx")
    part = lax.axis_index("pipe")
    ctx_pos = lax.axis_index("ctx")
    micro, rows, width = tokens.shape
    mine = rows // layers
    span = rows * tp_size
    slab = width // ctx_size
    gains = lax.all_gather(norm_gain[0], "pipe", axis=0)
    kv_rows = lax.dynamic_slice_in_dim(keyval_weight[0], ctx_pos * slab, slab, 0)
    project = swap_halves(query_weight[0], 1)
    kv_project = swap_halves(kv_rows, 1)
    q_cols = project.shape[2]
    project = jnp.concatenate([project, kv_project], axis=2)
    combine = swap_halves(output_weight[0], 0)
    kv_count = kv_project.shape[2] // (2 * HEAD_DIM)
    q_count = q_cols // HEAD_DIM
    positions = ctx_pos * span + jnp.arange(span, dtype=jnp.int32)
    outs = []
    for m in range(micro):
        state = lax.dynamic_slice_in_dim(tokens[m], part * mine, mine, 0)
        produced = []
        for layer in range(layers):
            wide = state.astype(jnp.float32)
            normed = normalize(wide, gains[layer].astype(jnp.float32))
            sliced = lax.all_to_all(normed.reshape(mine, ctx_size, slab), "ctx", 1, 0)
            sliced = sliced.reshape(ctx_size, mine, slab)
            everyone = lax.all_gather(sliced, ("tp", "pipe"), axis=1, tiled=True)
            everyone = everyone.reshape(ctx_size * span, slab)
            partial = jnp.dot(everyone, project[layer], preferred_element_type=jnp.float32)
            projected = lax.psum_scatter(
                partial.astype(jnp.bfloat16), "ctx", scatter_dimension=0, tiled=True
            ).astype(jnp.float32)
            query = rotate(projected[:, :q_cols].reshape(span, q_count, HEAD_DIM), positions)
            kv = projected[:, q_cols:].reshape(span, kv_count, 2, HEAD_DIM)
            kv = jnp.stack([rotate(kv[:, :, 0], positions), kv[:, :, 1]], axis=2)
            kv = lax.all_gather(
                kv.astype(jnp.bfloat16).reshape(span, kv_count * 2 * HEAD_DIM),
                "ctx",
                axis=0,
                tiled=True,
            ).reshape(ctx_size * span, kv_count, 2, HEAD_DIM)
            attended = attend(query.astype(jnp.bfloat16), kv[:, :, 0], kv[:, :, 1], positions)
            attended = lax.all_gather(attended, "ctx", axis=0, tiled=True)
            partial = jnp.dot(attended, combine[layer], preferred_element_type=jnp.float32)
            partial = partial.astype(jnp.bfloat16).reshape(ctx_size, span, slab)
            summed = lax.psum_scatter(
                partial, ("tp", "pipe"), scatter_dimension=1, tiled=True
            )
            summed = lax.all_to_all(summed, "ctx", 0, 1)
            summed = summed.reshape(mine, width).astype(jnp.float32)
            state = (wide + summed).astype(jnp.bfloat16)
            produced.append(state)
        outs.append(lax.all_to_all(jnp.stack(produced), "pipe", 0, 0).reshape(rows, width))
    return jnp.stack(outs)[None]


def per_device(tokens, norm_gain, query_weight, keyval_weight, output_weight):
    layers = lax.axis_size("pipe")
    kv_count = keyval_weight.shape[2] // (2 * HEAD_DIM)
    even = kv_count % layers == 0 and tokens.shape[1] % (16 * layers) == 0
    step = spread if even else gathered
    return step(tokens, norm_gain, query_weight, keyval_weight, output_weight)


def solution(mesh):
    in_specs = (
        P(None, ("ctx", "tp"), None),
        P("pipe", None),
        P("pipe", "ctx", "tp"),
        P("pipe", None, "tp"),
        P("pipe", "tp", "ctx"),
    )
    out_specs = P("pipe", None, ("ctx", "tp"), None)
    return jax.shard_map(
        per_device, mesh=mesh, in_specs=in_specs, out_specs=out_specs, check_vma=False
    )
```

```python
import functools
import math

import jax
import jax.numpy as jnp
from jax import lax
from jax.experimental import pallas as pl
from jax.experimental.pallas import tpu as pltpu
from jax.sharding import PartitionSpec as P

HEAD_DIM = 128


def shifted(value, axis, by):
    count = lax.axis_size(axis)
    pairs = [(i, i + by) for i in range(count) if 0 <= i + by < count]
    return lax.ppermute(value, axis, pairs)


def rotate(field, positions):
    half = field.shape[-1] // 2
    freqs = 500000.0 ** (-jnp.arange(half, dtype=jnp.float32) * 2.0 / field.shape[-1])
    angles = positions.astype(jnp.float32)[:, None] * freqs[None, :]
    cosine = jnp.cos(angles)[:, None, :]
    sine = jnp.sin(angles)[:, None, :]
    first = field[..., :half]
    second = field[..., half:]
    return jnp.concatenate(
        [first * cosine - second * sine, second * cosine + first * sine], axis=-1
    )


def normalize(block, scale_row):
    return (
        block * lax.rsqrt(jnp.mean(block * block, axis=-1, keepdims=True) + 1e-05) * scale_row
    ).astype(jnp.bfloat16)


def gathered(tokens, norm_gain, query_weight, keyval_weight, output_weight):
    segments = lax.axis_size("pipe")
    segment = lax.axis_index("pipe")
    tp_size = lax.axis_size("tp")
    ctx_pos = lax.axis_index("ctx")
    micro, rows, width = tokens.shape
    span = rows * tp_size
    scale_row = norm_gain[0].astype(jnp.float32)
    full_query, full_output = (
        lax.all_gather(query_weight[0], "ctx", axis=0, tiled=True),
        lax.all_gather(output_weight[0], "ctx", axis=1, tiled=True),
    )
    keyval = keyval_weight[0]
    q_count = full_query.shape[1] // HEAD_DIM
    kv_count = keyval.shape[1] // (2 * HEAD_DIM)
    group = q_count // kv_count
    positions = ctx_pos * span + jnp.arange(span, dtype=jnp.int32)
    factor = 1.0 / math.sqrt(HEAD_DIM)
    steps = micro + segments - 1
    received = jnp.zeros_like(tokens[0])
    results = []
    for step in range(steps):
        fresh = tokens[min(step, micro - 1)]
        state = jnp.where(segment == 0, fresh, received)
        wide = state.astype(jnp.float32)
        layer_normed = lax.all_gather(normalize(wide, scale_row), "tp", axis=0, tiled=True)
        query = jnp.dot(layer_normed, full_query, preferred_element_type=jnp.float32).reshape(
            span, q_count, HEAD_DIM
        )
        query = rotate(query, positions).astype(jnp.bfloat16)
        query = query.reshape(span, kv_count, group, HEAD_DIM).transpose(1, 2, 0, 3)
        projected = jnp.dot(layer_normed, keyval, preferred_element_type=jnp.float32).reshape(
            span, kv_count, 2, HEAD_DIM
        )
        keys = (
            rotate(projected[:, :, 0], positions)
            .astype(jnp.bfloat16)
            .reshape(span, kv_count * HEAD_DIM)
        )
        values = projected[:, :, 1].astype(jnp.bfloat16).reshape(span, kv_count * HEAD_DIM)
        piece = (
            lax.all_gather(keys, "ctx", axis=0, tiled=True),
            lax.all_gather(values, "ctx", axis=0, tiled=True),
        )
        run_max = jnp.full((kv_count, group, span), -1e30, jnp.float32)
        count = piece[0].shape[0]
        key_block = piece[0].reshape(count, kv_count, HEAD_DIM)
        value_block = piece[1].reshape(count, kv_count, HEAD_DIM)
        scores = (
            jnp.einsum("hgqd,khd->hgqk", query, key_block, preferred_element_type=jnp.float32)
            * factor
        )
        key_pos = jnp.arange(count, dtype=jnp.int32)
        allowed = key_pos[None, :] <= positions[:, None]
        scores = jnp.where(allowed, scores, -jnp.inf)
        new_max = jnp.maximum(run_max, jnp.max(scores, axis=-1))
        weights = jnp.exp(scores - new_max[..., None])
        total = jnp.sum(weights, axis=-1)
        mixed = jnp.einsum(
            "hgqk,khd->hgqd",
            weights.astype(jnp.bfloat16),
            value_block,
            preferred_element_type=jnp.float32,
        )
        run_max = new_max
        run_acc = mixed
        mixed = run_acc / total[..., None]
        attended = (
            mixed.transpose(2, 0, 1, 3).reshape(span, q_count * HEAD_DIM).astype(jnp.bfloat16)
        )
        summed = lax.psum_scatter(
            jnp.dot(attended, full_output, preferred_element_type=jnp.float32).astype(jnp.bfloat16),
            "tp",
            scatter_dimension=0,
            tiled=True,
        ).astype(jnp.float32)
        produced = (wide + summed).astype(jnp.bfloat16)
        results.append(produced)
        if step + 1 < steps:
            received = shifted(produced, "pipe", 1)
    stacked = jnp.stack(results)
    mine = lax.dynamic_slice_in_dim(stacked, segment, micro, 0)
    return mine[None]


MESH = pl.DeviceIdType.MESH


def neighbours():
    count = lax.axis_size("ctx") // 2
    here = lax.axis_index("ctx")
    row = here // 2
    side = here % 2
    return count, here, row, side, here + 1 - 2 * side


def greet(count, here, row, partner):
    barrier = pltpu.get_barrier_semaphore()
    pl.semaphore_signal(barrier, inc=1, device_id={"ctx": partner}, device_id_type=MESH)

    @pl.when(row + 1 < count)
    def _():
        pl.semaphore_signal(barrier, inc=1, device_id={"ctx": here + 2}, device_id_type=MESH)

    @pl.when(row >= 1)
    def _():
        pl.semaphore_signal(barrier, inc=1, device_id={"ctx": here - 2}, device_id_type=MESH)

    pl.semaphore_wait(barrier, 1 + (row + count - 1) // count + (2 * count - 2 - row) // count)


def gather_kernel(cut, in_ref, out_ref, send_sem, recv_sem):
    count, here, row, side, partner = neighbours()
    rows = in_ref.shape[0]
    pieces = (pl.ds(0, cut), pl.ds(cut, rows - cut))
    greet(count, here, row, partner)
    has_up = row + 1 < count
    has_down = row >= 1

    def copy(block, half, way, own=False):
        target = (here + 2, here - 2, partner)[way]
        there = out_ref.at[block, pieces[half]]
        return pltpu.make_async_remote_copy(
            src_ref=in_ref.at[pieces[half]] if own else there,
            dst_ref=there,
            send_sem=send_sem.at[block, half, way],
            recv_sem=recv_sem.at[block, half],
            device_id={"ctx": target},
            device_id_type=MESH,
        )

    def arrive(block, half):
        copy(block, half, 2).wait_recv()

    sends = []

    def send(cond, block, half, way, own=False):
        sends.append((cond, block, half, way, own))

        @pl.when(cond)
        def _():
            copy(block, half, way, own).start()

    always = row >= 0
    send(always, here, 1, 2, True)
    for half in (1, 0):
        send(has_up, here, half, 0, True)
        send(has_down, here, half, 1, True)
    send(always, here, 0, 2, True)
    out_ref[here] = in_ref[...]
    arrive(partner, 1)
    send(has_up, partner, 1, 0)
    send(has_down, partner, 1, 1)
    for j in range(1, count):
        below = row >= j
        above = row + j < count
        for half, away in ((0, 0), (1, 0), (1, 1)):
            for near, step, way, onward in ((below, -2 * j, 0, has_up), (above, 2 * j, 1, has_down)):
                block = (here if away == 0 else partner) + step

                @pl.when(near)
                def _():
                    arrive(block, half)

                send(jnp.logical_and(near, onward), block, half, way)
                if half == 0:
                    send(near, block, half, 2)
    arrive(partner, 0)
    for j in range(1, count):
        for near, step in ((row >= j, -2 * j), (row + j < count, 2 * j)):

            @pl.when(near)
            def _():
                arrive(partner + step, 0)

    for cond, block, half, way, own in sends:

        @pl.when(cond)
        def _():
            copy(block, half, way, own).wait_send()


def ctx_gather(value, number):
    rows, columns = value.shape
    blocks = lax.axis_size("ctx")
    gathered_value = pl.pallas_call(
        functools.partial(gather_kernel, rows // 2),
        out_shape=jax.ShapeDtypeStruct((blocks, rows, columns), value.dtype),
        in_specs=[pl.BlockSpec(memory_space=pltpu.VMEM)],
        out_specs=pl.BlockSpec(memory_space=pltpu.VMEM),
        scratch_shapes=[
            pltpu.SemaphoreType.DMA((blocks, 2, 3)),
            pltpu.SemaphoreType.DMA((blocks, 2)),
        ],
        compiler_params=pltpu.CompilerParams(collective_id=number, has_side_effects=True),
    )(value)
    return gathered_value.reshape(blocks * rows, columns)


def scatter_kernel(
    cut, in_ref, out_ref, cross, sums, up_in, down_in, z_sums, z_up, z_down, z_cross, z_last,
    x_send, x_recv, b_send, b_recv, a_send, a_recv, l_send, l_recv,
):
    count, here, row, side, partner = neighbours()
    rows = in_ref.shape[1]
    first, second = pl.ds(0, cut), pl.ds(cut, rows - cut)
    greet(count, here, row, partner)
    has_up = row + 1 < count
    has_down = row >= 1
    order = []
    for j in range(count - 1, 0, -1):
        order.append((row + j < count, row + j, 0))
        order.append((row >= j, row - j, 1))
    always = row >= 0

    def remote(src, dst, send, recv, target):
        return pltpu.make_async_remote_copy(
            src_ref=src, dst_ref=dst, send_sem=send, recv_sem=recv,
            device_id={"ctx": target}, device_id_type=MESH,
        )

    def over(dest):
        return remote(
            in_ref.at[2 * dest + 1 - side, second], cross.at[dest],
            x_send.at[dest], x_recv.at[dest], partner,
        )

    def chain_b(dest, way):
        return remote(
            sums.at[dest], (up_in, down_in)[way].at[dest],
            b_send.at[dest], b_recv.at[way, dest], (here + 2, here - 2)[way],
        )

    def chain_a(dest, way, x):
        return remote(
            z_sums.at[dest, x], (z_up, z_down)[way].at[dest, x],
            a_send.at[dest, x], a_recv.at[way, dest, x], (here + 2, here - 2)[way],
        )

    last = remote(z_cross, z_last, l_send.at[0], l_recv.at[0], partner)

    def wide(value):
        return value.astype(jnp.float32)

    for cond, dest, way in order + [(always, row, 0)]:

        @pl.when(cond)
        def _():
            over(dest).start()

    for cond, dest, way in order:
        behind = (has_down, has_up)[way]
        for x in range(2):

            @pl.when(jnp.logical_and(cond, behind))
            def _():
                chain_a(dest, way, x).wait_recv()
                z_sums[dest, x] = (
                    wide(in_ref[2 * dest + x, first]) + wide((z_up, z_down)[way][dest, x])
                ).astype(jnp.bfloat16)

            @pl.when(jnp.logical_and(cond, jnp.logical_not(behind)))
            def _():
                z_sums[dest, x] = in_ref[2 * dest + x, first]

            @pl.when(cond)
            def _():
                chain_a(dest, way, x).start()

        @pl.when(cond)
        def _():
            over(dest).wait_recv()

        @pl.when(jnp.logical_and(cond, behind))
        def _():
            chain_b(dest, way).wait_recv()
            sums[dest] = (
                wide(in_ref[2 * dest + side, second])
                + wide(cross[dest])
                + wide((up_in, down_in)[way][dest])
            ).astype(jnp.bfloat16)

        @pl.when(jnp.logical_and(cond, jnp.logical_not(behind)))
        def _():
            sums[dest] = (wide(in_ref[2 * dest + side, second]) + wide(cross[dest])).astype(jnp.bfloat16)

        @pl.when(cond)
        def _():
            chain_b(dest, way).start()

    @pl.when(has_down)
    def _():
        chain_a(row, 0, 0).wait_recv()
        chain_a(row, 0, 1).wait_recv()

    @pl.when(jnp.logical_not(has_down))
    def _():
        z_up[row] = jnp.zeros_like(z_up[row])
        up_in[row] = jnp.zeros_like(up_in[row])

    @pl.when(has_up)
    def _():
        chain_a(row, 1, 0).wait_recv()
        chain_a(row, 1, 1).wait_recv()

    @pl.when(jnp.logical_not(has_up))
    def _():
        z_down[row] = jnp.zeros_like(z_down[row])
        down_in[row] = jnp.zeros_like(down_in[row])

    z_cross[...] = (
        wide(in_ref[partner, first]) + wide(z_up[row, 1 - side]) + wide(z_down[row, 1 - side])
    ).astype(jnp.bfloat16)
    last.start()
    over(row).wait_recv()

    @pl.when(has_down)
    def _():
        chain_b(row, 0).wait_recv()

    @pl.when(has_up)
    def _():
        chain_b(row, 1).wait_recv()

    out_ref[second] = (
        wide(in_ref[here, second]) + wide(cross[row]) + wide(up_in[row]) + wide(down_in[row])
    )
    last.wait_recv()
    out_ref[first] = (
        wide(in_ref[here, first]) + wide(z_up[row, side]) + wide(z_down[row, side]) + wide(z_last[...])
    )
    for cond, dest, way in order + [(always, row, 0)]:

        @pl.when(cond)
        def _():
            over(dest).wait_send()

    for cond, dest, way in order:

        @pl.when(cond)
        def _():
            chain_a(dest, way, 0).wait_send()
            chain_a(dest, way, 1).wait_send()
            chain_b(dest, way).wait_send()

    last.wait_send()


def ctx_scatter(partial, number):
    blocks, rows, columns = partial.shape
    count = blocks // 2
    cut = rows * 3 // 8 // 16 * 16
    rest = rows - cut
    kind = partial.dtype
    return pl.pallas_call(
        functools.partial(scatter_kernel, cut),
        out_shape=jax.ShapeDtypeStruct((rows, columns), jnp.float32),
        in_specs=[pl.BlockSpec(memory_space=pltpu.VMEM)],
        out_specs=pl.BlockSpec(memory_space=pltpu.VMEM),
        scratch_shapes=[pltpu.VMEM((count, rest, columns), kind)] * 4
        + [pltpu.VMEM((count, 2, cut, columns), kind)] * 3
        + [pltpu.VMEM((cut, columns), kind)] * 2
        + [
            pltpu.SemaphoreType.DMA((count,)),
            pltpu.SemaphoreType.DMA((count,)),
            pltpu.SemaphoreType.DMA((count,)),
            pltpu.SemaphoreType.DMA((2, count)),
            pltpu.SemaphoreType.DMA((count, 2)),
            pltpu.SemaphoreType.DMA((2, count, 2)),
            pltpu.SemaphoreType.DMA((1,)),
            pltpu.SemaphoreType.DMA((1,)),
        ],
        compiler_params=pltpu.CompilerParams(collective_id=number, has_side_effects=True),
    )(partial)


def swap_halves(weight, axis):
    segments = lax.axis_size("pipe")
    shape = weight.shape
    split = shape[:axis] + (segments, shape[axis] // segments) + shape[axis + 1 :]
    blocks = jnp.moveaxis(weight.reshape(split), axis, 0)
    return lax.all_to_all(blocks, "pipe", 0, 0)


def attend(query, keys, values, positions):
    span, q_count, _ = query.shape
    kv_count = keys.shape[1]
    group = q_count // kv_count
    query = query.reshape(span, kv_count, group, HEAD_DIM).transpose(1, 2, 0, 3)
    scores = jnp.einsum("hgqd,khd->hgqk", query, keys, preferred_element_type=jnp.float32)
    scores = scores * (1.0 / math.sqrt(HEAD_DIM))
    allowed = jnp.arange(keys.shape[0], dtype=jnp.int32)[None, :] <= positions[:, None]
    scores = jnp.where(allowed, scores, -jnp.inf)
    weights = jnp.exp(scores - jnp.max(scores, axis=-1, keepdims=True))
    total = jnp.sum(weights, axis=-1, keepdims=True)
    mixed = jnp.einsum(
        "hgqk,khd->hgqd",
        weights.astype(jnp.bfloat16),
        values,
        preferred_element_type=jnp.float32,
    )
    mixed = (mixed / total).astype(jnp.bfloat16)
    return mixed.transpose(2, 0, 1, 3).reshape(span, q_count * HEAD_DIM)


def spread(tokens, norm_gain, query_weight, keyval_weight, output_weight):
    layers = lax.axis_size("pipe")
    tp_size = lax.axis_size("tp")
    ctx_size = lax.axis_size("ctx")
    part = lax.axis_index("pipe")
    ctx_pos = lax.axis_index("ctx")
    micro, rows, width = tokens.shape
    mine = rows // layers
    span = rows * tp_size
    slab = width // ctx_size
    gains = lax.all_gather(norm_gain[0], "pipe", axis=0)
    kv_rows = lax.dynamic_slice_in_dim(keyval_weight[0], ctx_pos * slab, slab, 0)
    project = swap_halves(query_weight[0], 1)
    kv_project = swap_halves(kv_rows, 1)
    q_cols = project.shape[2]
    project = jnp.concatenate([project, kv_project], axis=2)
    combine = swap_halves(output_weight[0], 0)
    kv_count = kv_project.shape[2] // (2 * HEAD_DIM)
    q_count = q_cols // HEAD_DIM
    positions = ctx_pos * span + jnp.arange(span, dtype=jnp.int32)
    outs = []
    for m in range(micro):
        state = lax.dynamic_slice_in_dim(tokens[m], part * mine, mine, 0)
        produced = []
        for layer in range(layers):
            wide = state.astype(jnp.float32)
            normed = normalize(wide, gains[layer].astype(jnp.float32))
            sliced = lax.all_to_all(normed.reshape(mine, ctx_size, slab), "ctx", 1, 0)
            sliced = sliced.reshape(ctx_size, mine, slab)
            everyone = lax.all_gather(sliced, ("tp", "pipe"), axis=1, tiled=True)
            everyone = everyone.reshape(ctx_size * span, slab)
            partial = jnp.dot(everyone, project[layer], preferred_element_type=jnp.float32)
            projected = ctx_scatter(
                partial.astype(jnp.bfloat16).reshape(ctx_size, span, partial.shape[1]), 0
            )
            query = rotate(projected[:, :q_cols].reshape(span, q_count, HEAD_DIM), positions)
            kv = projected[:, q_cols:].reshape(span, kv_count, 2, HEAD_DIM)
            kv = jnp.stack([rotate(kv[:, :, 0], positions), kv[:, :, 1]], axis=2)
            kv = ctx_gather(
                kv.astype(jnp.bfloat16).reshape(span, kv_count * 2 * HEAD_DIM), 1
            ).reshape(ctx_size * span, kv_count, 2, HEAD_DIM)
            attended = attend(query.astype(jnp.bfloat16), kv[:, :, 0], kv[:, :, 1], positions)
            attended = ctx_gather(attended, 2)
            partial = jnp.dot(attended, combine[layer], preferred_element_type=jnp.float32)
            partial = partial.astype(jnp.bfloat16).reshape(ctx_size, span, slab)
            summed = lax.psum_scatter(
                partial, ("tp", "pipe"), scatter_dimension=1, tiled=True
            )
            summed = lax.all_to_all(summed, "ctx", 0, 1)
            summed = summed.reshape(mine, width).astype(jnp.float32)
            state = (wide + summed).astype(jnp.bfloat16)
            produced.append(state)
        outs.append(lax.all_to_all(jnp.stack(produced), "pipe", 0, 0).reshape(rows, width))
    return jnp.stack(outs)[None]


def per_device(tokens, norm_gain, query_weight, keyval_weight, output_weight):
    layers = lax.axis_size("pipe")
    kv_count = keyval_weight.shape[2] // (2 * HEAD_DIM)
    even = lax.axis_size("ctx") % 2 == 0 and kv_count % layers == 0 and tokens.shape[1] % (16 * layers) == 0
    step = spread if even else gathered
    return step(tokens, norm_gain, query_weight, keyval_weight, output_weight)


def solution(mesh):
    in_specs = (
        P(None, ("ctx", "tp"), None),
        P("pipe", None),
        P("pipe", "ctx", "tp"),
        P("pipe", None, "tp"),
        P("pipe", "tp", "ctx"),
    )
    out_specs = P("pipe", None, ("ctx", "tp"), None)
    return jax.shard_map(
        per_device, mesh=mesh, in_specs=in_specs, out_specs=out_specs, check_vma=False
    )
```
